32 devices in a mesh: groups: 2 (over x), rows: 16 (over z, y, core).
Axes of the slice: x: 2, y: 2, z: 4, core: 2. Of those that a mesh axis runs over, the one named last changes fastest.
Arguments:
- features: bfloat16 [32768, 384], P(('groups', 'rows')), parts along dimension 0, may hold values from -8 to 8
- iterate: float32 [32768, 64], P(('groups', 'rows')), parts along dimension 0, may hold values from -6 to 6
- band_mask: int32 [32, 2], P(('groups', 'rows')), parts along dimension 0, may hold values from 0 to 1, as said below
Outputs:
- eigvecs: float32 [32768, 64], P(('groups', 'rows')), parts along dimension 0
- degrees: float32 [32768], P(('groups', 'rows')), parts along dimension 0
The draws below stay inside these ranges and needn't reach their ends.
There are 2 independent parts, one for each index of `groups`. The reference program is written for one: setup_inputs(seed, part) draws one part's arguments, and reference() takes and returns one part's arrays. A program takes and returns all parts, laid end to end along the dimension named above; each array names one. Nothing has to cross between parts.
Inputs may be any that keep to these rules, and one draw needn't show every extreme that they name: band_mask[i, o] is 0 wherever i + o + 1 >= 16, and 1 wherever i + o + 1 == 15.
All inputs are finite; a program needn't handle non-finite values.
Results may differ from the reference program's by a relative error of at most 0.0067.
Values may be sent and summed in bfloat16 or wider, within the bound.
A program may use at most 64 MiB of HBM per device.

```python
import jax
import jax.numpy as jnp
from jax import lax

C = 384
K = 64
W = 2
ITERS = 2
BLK = 1024
NBLK = 16
TOKENS = 16384


def draw_band_mask(key, part):
    values = jax.random.randint(key, (NBLK, W), 0, 3)
    block_index = jnp.arange(NBLK, dtype=jnp.int32)[:, None]
    offset = jnp.arange(W, dtype=jnp.int32)[None, :] + 1
    inside = block_index + offset < NBLK
    last_touch = block_index + offset == NBLK - 1
    return jnp.where(inside & ((values > 0) | last_touch), 1, 0).astype(jnp.int32)


def draw_features(key, part):
    spread_count = max(BLK // 512, 1)
    centre_key, choose_key, flip_key, weight_key, jitter_key = jax.random.split(jax.random.fold_in(key, 7), 5)
    centres = jax.random.normal(centre_key, (NBLK * spread_count + 2 * spread_count, C), jnp.float32)
    block_of = jnp.arange(TOKENS, dtype=jnp.int32) // BLK
    chosen = block_of * spread_count + jax.random.randint(choose_key, (TOKENS,), 0, 3 * spread_count)
    sign_flip = (2 * jax.random.randint(flip_key, (TOKENS,), 0, 2) - 1).astype(jnp.float32)
    weights = jax.random.uniform(weight_key, (TOKENS,), jnp.float32, 0.7, 0.97)
    jitter = jax.random.normal(jitter_key, (TOKENS, C), jnp.float32)
    remainder = jnp.sqrt(1.0 - weights * weights)
    values = (sign_flip * weights)[:, None] * centres[chosen] + remainder[:, None] * jitter
    return jnp.clip(values, -8.0, 8.0).astype(jnp.bfloat16)


def block_scale(own_key, extent, cuts, smallest, high):
    def one(axis_at, blocks):
        steps = jax.random.uniform(jax.random.fold_in(jax.random.fold_in(own_key, 6), axis_at), (blocks,), jnp.float32, smallest / len(cuts), high / len(cuts))
        return jnp.repeat(jnp.exp(steps), extent[axis_at] // blocks).reshape((-1,) + (1,) * (len(extent) - axis_at - 1))

    factor_of = one(*cuts[0])
    for cut in cuts[1:]:
        factor_of = factor_of * one(*cut)
    return factor_of


def noise(key, dims, scale, limit, shards=(), held_as=jnp.bfloat16):
    gain = block_scale(key, dims, shards, -0.22, 0.18) if shards else 1.0
    values = jax.random.normal(key, dims, jnp.float32) * scale * gain
    return jnp.minimum(jnp.maximum(values, -limit), limit).astype(held_as)


def setup_inputs(seed: int = 0, part: int = 0) -> dict:
    splits = jax.random.split(jax.random.key(seed), 4)
    part_keys = jax.random.split(jax.random.fold_in(splits[3], part), 4)
    features = draw_features(jax.random.fold_in(jax.random.fold_in(splits[3], part), 71), part)
    iterate = noise(part_keys[1], (TOKENS, K), 1.0, 6.0, ((0, 16),), jnp.float32)
    band_mask = draw_band_mask(jax.random.fold_in(jax.random.fold_in(splits[3], part), 71), part)
    return {"features": features, "iterate": iterate, "band_mask": band_mask}


def unit_rows(features):
    values = features.astype(jnp.float32)
    return (values * lax.rsqrt(lax.optimization_barrier(jnp.sum(values * values, axis=-1, keepdims=True)) + 1e-06)).astype(jnp.bfloat16)

def affinity(left, right):
    count = left.shape[0]
    step = min(512, count)
    pieces = []
    for start in range(0, count, step):
        scores = lax.dot_general(left[start:start + step].astype(jnp.float32), right.astype(jnp.float32), (((1,), (1,)), ((), ())), preferred_element_type=jnp.float32)
        pieces.append(jnp.exp(scores).astype(jnp.bfloat16))
    return jnp.concatenate(pieces, 0)

def spread(own, mirrored):
    total = own
    for offset in range(1, W + 1):
        moved = jnp.concatenate([jnp.zeros_like(mirrored[:offset, offset - 1]), mirrored[:NBLK - offset, offset - 1]], 0)
        total = total + moved
    return total

def reference(features, iterate, band_mask):
    unit = unit_rows(features)

    def form(index):
        left = lax.dynamic_slice_in_dim(unit, index * BLK, BLK, 0)
        tiles = [affinity(left, left)]
        for offset in range(1, W + 1):
            where = (jnp.minimum(index + offset, NBLK - 1) * BLK).astype(jnp.int32)
            right = lax.dynamic_slice_in_dim(unit, where, BLK, 0)
            keep = band_mask[index, offset - 1].astype(jnp.bfloat16)
            tiles.append(affinity(left, right) * keep)
        return jnp.stack(tiles)
    blocks = jnp.arange(NBLK, dtype=jnp.int32)
    tiles = lax.map(form, blocks)

    def degree_terms(index):
        tile_set = tiles[index]
        own = lax.optimization_barrier(jnp.sum(tile_set[0].astype(jnp.float32), axis=1))
        mirrored = []
        for offset in range(1, W + 1):
            own = own + lax.optimization_barrier(jnp.sum(tile_set[offset].astype(jnp.float32), axis=1))
            mirrored.append(lax.optimization_barrier(jnp.sum(tile_set[offset].astype(jnp.float32), axis=0)))
        return (own, jnp.stack(mirrored))
    own_deg, mirr_deg = lax.map(degree_terms, blocks)
    degrees = spread(own_deg, mirr_deg).reshape(TOKENS)
    scale = lax.rsqrt(degrees)[:, None]
    current = iterate
    for step in range(ITERS):
        scaled = (current * scale).astype(jnp.bfloat16)

        def product_terms(index):
            tile_set = tiles[index]
            own_vec = lax.dynamic_slice_in_dim(scaled, index * BLK, BLK, 0)
            rows_sum = jnp.dot(tile_set[0].astype(jnp.float32), own_vec.astype(jnp.float32), preferred_element_type=jnp.float32)
            mirrored = []
            for offset in range(1, W + 1):
                where = (jnp.minimum(index + offset, NBLK - 1) * BLK).astype(jnp.int32)
                partner = lax.dynamic_slice_in_dim(scaled, where, BLK, 0)
                rows_sum = rows_sum + jnp.dot(tile_set[offset].astype(jnp.float32), partner.astype(jnp.float32), preferred_element_type=jnp.float32)
                mirrored.append(lax.dot_general(tile_set[offset].astype(jnp.float32), own_vec.astype(jnp.float32), (((0,), (0,)), ((), ())), preferred_element_type=jnp.float32))
            return (rows_sum, jnp.stack(mirrored))
        own_terms, mirr_terms = lax.map(product_terms, blocks)
        image = spread(own_terms, mirr_terms).reshape(TOKENS, K)
        normed = image * scale
        gram = jnp.dot(normed.T.astype(jnp.float32), normed.astype(jnp.float32), precision=lax.Precision.HIGHEST, preferred_element_type=jnp.float32)
        lower = jnp.linalg.cholesky(gram)
        current = jax.scipy.linalg.solve_triangular(lower, normed.T, lower=True).T
    return (current, degrees)
```

```python
import functools

import jax
import jax.numpy as jnp
from jax import lax
from jax.experimental import pallas as pl
from jax.experimental.pallas import tpu as pltpu
from jax.sharding import PartitionSpec as P

W = 2
ITERS = 2
AXIS = "rows"
MESH = pl.DeviceIdType.MESH
HIGH = lax.Precision.HIGHEST


def radices(count):
    out = []
    while count > 1:
        radix = next((r for r in (4, 2, 3, 5, 7) if count % r == 0), count)
        out.append(radix)
        count //= radix
    return out


def peers_of(me, plan):
    stride = 1
    found = []
    for radix in plan:
        digit = lax.rem(lax.div(me, stride), radix)
        row = []
        for k in range(1, radix):
            other = lax.rem(digit + k, radix)
            row.append((other, me + (other - digit) * stride))
        found.append((digit, row))
        stride *= radix
    return found


def all_sum(value, found, box, send_sem, recv_sem):
    for phase, (digit, row) in enumerate(found):
        box[phase, digit] = value
        copies = []
        for k, (other, peer) in enumerate(row):
            copy = pltpu.make_async_remote_copy(
                src_ref=box.at[phase, digit],
                dst_ref=box.at[phase, digit],
                send_sem=send_sem.at[phase, k],
                recv_sem=recv_sem.at[phase, digit],
                device_id={AXIS: peer},
                device_id_type=MESH,
            )
            copy.start()
            copies.append(copy)
        for other, peer in row:
            pltpu.make_async_remote_copy(
                src_ref=box.at[phase, other],
                dst_ref=box.at[phase, other],
                send_sem=send_sem.at[phase, 0],
                recv_sem=recv_sem.at[phase, other],
                device_id={AXIS: peer},
                device_id_type=MESH,
            ).wait_recv()
        value = box[phase, 0]
        for slot in range(1, len(row) + 1):
            value = value + box[phase, slot]
        for copy in copies:
            copy.wait_send()
    return value


def inverse_factor(gram):
    size = gram.shape[0]
    rows = lax.broadcasted_iota(jnp.int32, (size, size), 0)
    cols = lax.broadcasted_iota(jnp.int32, (size, size), 1)
    both = jnp.concatenate([gram, jnp.where(rows == cols, 1.0, 0.0)], axis=1)
    count = size // 8
    bands = [both[8 * b : 8 * b + 8] for b in range(count)]
    sub = lax.broadcasted_iota(jnp.int32, (8, 1), 0)
    pivots = []
    for j in range(size):
        b, s = j // 8, j % 8
        row = bands[b][s : s + 1]
        pivot = row[:, j : j + 1]
        pivots.append(pivot)
        scaled = row * (1.0 / pivot)
        for c in range(b, count):
            column = bands[c][:, j : j + 1]
            if c == b:
                column = jnp.where(sub > s, column, 0.0)
            bands[c] = bands[c] - column * scaled
    out = []
    for b in range(count):
        diagonal = jnp.zeros((8, 1), jnp.float32)
        for s in range(8):
            diagonal = jnp.where(sub == s, pivots[8 * b + s], diagonal)
        out.append(bands[b][:, size:] * lax.rsqrt(diagonal))
    return jnp.concatenate(out, axis=0)


def pack(gram):
    half = gram.shape[0] // 2
    return jnp.concatenate([gram[:half], gram[half:]], axis=1)


def unpack(packed):
    size = packed.shape[1] // 2
    return jnp.concatenate([packed[:, :size], packed[:, size:]], axis=0)


def ortho_kernel(plan, image_ref, scale_ref, out_ref, box, send_sem, recv_sem):
    me = lax.axis_index(AXIS)
    found = peers_of(me, plan)
    barrier = pltpu.get_barrier_semaphore()
    total = 0
    for _, row in found:
        for _, peer in row:
            pl.semaphore_signal(barrier, inc=1, device_id={AXIS: peer}, device_id_type=MESH)
            total += 1
    normed = image_ref[...] * scale_ref[...]
    gram = lax.dot_general(
        normed, normed, (((0,), (0,)), ((), ())), precision=HIGH, preferred_element_type=jnp.float32
    )
    pl.semaphore_wait(barrier, total)
    gram = unpack(all_sum(pack(gram), found, box, send_sem, recv_sem))
    inverse = inverse_factor(gram)
    out_ref[...] = lax.dot_general(
        normed, inverse, (((1,), (1,)), ((), ())), precision=HIGH, preferred_element_type=jnp.float32
    )


def ortho(image, scale, peers):
    size = image.shape[1]
    plan = radices(peers)
    return pl.pallas_call(
        functools.partial(ortho_kernel, plan),
        out_shape=jax.ShapeDtypeStruct(image.shape, jnp.float32),
        in_specs=[pl.BlockSpec(memory_space=pltpu.VMEM)] * 2,
        out_specs=pl.BlockSpec(memory_space=pltpu.VMEM),
        scratch_shapes=[
            pltpu.VMEM((len(plan), max(plan), size // 2, 2 * size), jnp.float32),
            pltpu.SemaphoreType.DMA((len(plan), max(plan))),
            pltpu.SemaphoreType.DMA((len(plan), max(plan))),
        ],
        compiler_params=pltpu.CompilerParams(collective_id=0, has_side_effects=True),
        name="ortho",
    )(image, scale)


def shifted(array, axis, by):
    peers = lax.axis_size(axis)
    pairs = [(i, i + by) for i in range(peers) if 0 <= i + by < peers]
    return lax.ppermute(array, axis, pairs)


def unit_rows(features):
    values = features.astype(jnp.float32)
    return (values * lax.rsqrt(jnp.sum(values * values, axis=-1, keepdims=True) + 1e-06)).astype(
        jnp.bfloat16
    )


def affinity(left, right):
    count = left.shape[0]
    step = min(512, count)
    pieces = []
    for start in range(0, count, step):
        scores = lax.dot_general(
            left[start : start + step],
            right,
            (((1,), (1,)), ((), ())),
            preferred_element_type=jnp.float32,
        )
        pieces.append(jnp.exp(scores).astype(jnp.bfloat16))
    return jnp.concatenate(pieces, 0)


def local(peers, features, iterate, band_mask):
    unit = unit_rows(features)
    keep_row = band_mask[0]
    reach = W
    partners = []
    for offset in range(1, reach + 1):
        partners.append(shifted(unit, "rows", -offset))
    tiles = [affinity(unit, unit)]
    for offset in range(1, reach + 1):
        keep = keep_row[offset - 1]
        partner = partners[offset - 1]
        tiles.append(affinity(unit, partner) * keep.astype(jnp.bfloat16))
    degrees = jnp.sum(tiles[0].astype(jnp.float32), axis=1)
    for offset in range(1, reach + 1):
        degrees = degrees + jnp.sum(tiles[offset].astype(jnp.float32), axis=1)
    for offset in range(1, reach + 1):
        column_sums = jnp.sum(tiles[offset].astype(jnp.float32), axis=0)
        degrees = degrees + shifted(column_sums, "rows", offset)
    scale = lax.rsqrt(degrees)[:, None]
    current = iterate
    for step in range(ITERS):
        scaled = (current * scale).astype(jnp.bfloat16)
        neighbours = []
        for offset in range(1, reach + 1):
            neighbours.append(shifted(scaled, "rows", -offset))
        image = jnp.dot(tiles[0], scaled, preferred_element_type=jnp.float32)
        for offset in range(1, reach + 1):
            image = image + jnp.dot(
                tiles[offset], neighbours[offset - 1], preferred_element_type=jnp.float32
            )
        for offset in range(1, reach + 1):
            mirrored = lax.dot_general(
                tiles[offset], scaled, (((0,), (0,)), ((), ())), preferred_element_type=jnp.float32
            )
            image = image + shifted(mirrored, "rows", offset)
        current = ortho(image, scale, peers)
    return (current, degrees)


def solution(mesh):
    return jax.shard_map(
        functools.partial(local, mesh.shape[AXIS]),
        mesh=mesh,
        in_specs=(
            P(("groups", "rows"), None),
            P(("groups", "rows"), None),
            P(("groups", "rows"), None),
        ),
        out_specs=(P(("groups", "rows"), None), P(("groups", "rows"))),
        check_vma=False,
    )
```

```python
import functools

import jax
import jax.numpy as jnp
from jax import lax
from jax.experimental import pallas as pl
from jax.experimental.pallas import tpu as pltpu
from jax.sharding import PartitionSpec as P

W = 2
ITERS = 2
AXIS = "rows"
MESH = pl.DeviceIdType.MESH
HIGH = lax.Precision.HIGHEST


def radices(count):
    out = []
    while count > 1:
        radix = next((r for r in (4, 2, 3, 5, 7) if count % r == 0), count)
        out.append(radix)
        count //= radix
    return out


def peers_of(me, plan):
    stride = 1
    found = []
    for radix in plan:
        digit = lax.rem(lax.div(me, stride), radix)
        row = []
        for k in range(1, radix):
            other = lax.rem(digit + k, radix)
            row.append((other, me + (other - digit) * stride))
        found.append((digit, row))
        stride *= radix
    return found


def all_sum(value, found, box, send_sem, recv_sem):
    for phase, (digit, row) in enumerate(found):
        box[phase, digit] = value
        copies = []
        for k, (other, peer) in enumerate(row):
            copy = pltpu.make_async_remote_copy(
                src_ref=box.at[phase, digit],
                dst_ref=box.at[phase, digit],
                send_sem=send_sem.at[phase, k],
                recv_sem=recv_sem.at[phase, digit],
                device_id={AXIS: peer},
                device_id_type=MESH,
            )
            copy.start()
            copies.append(copy)
        for other, peer in row:
            pltpu.make_async_remote_copy(
                src_ref=box.at[phase, other],
                dst_ref=box.at[phase, other],
                send_sem=send_sem.at[phase, 0],
                recv_sem=recv_sem.at[phase, other],
                device_id={AXIS: peer},
                device_id_type=MESH,
            ).wait_recv()
        value = box[phase, 0]
        for slot in range(1, len(row) + 1):
            value = value + box[phase, slot]
        for copy in copies:
            copy.wait_send()
    return value


def inverse_factor(gram):
    size = gram.shape[0]
    rows = lax.broadcasted_iota(jnp.int32, (size, size), 0)
    cols = lax.broadcasted_iota(jnp.int32, (size, size), 1)
    both = jnp.concatenate([gram, jnp.where(rows == cols, 1.0, 0.0)], axis=1)
    count = size // 8
    bands = [both[8 * b : 8 * b + 8] for b in range(count)]
    sub = lax.broadcasted_iota(jnp.int32, (8, 1), 0)
    pivots = []
    for j in range(size):
        b, s = j // 8, j % 8
        row = bands[b][s : s + 1]
        pivot = row[:, j : j + 1]
        pivots.append(pivot)
        scaled = row * (1.0 / pivot)
        for c in range(b, count):
            column = bands[c][:, j : j + 1]
            if c == b:
                column = jnp.where(sub > s, column, 0.0)
            bands[c] = bands[c] - column * scaled
    out = []
    for b in range(count):
        diagonal = jnp.zeros((8, 1), jnp.float32)
        for s in range(8):
            diagonal = jnp.where(sub == s, pivots[8 * b + s], diagonal)
        out.append(bands[b][:, size:] * lax.rsqrt(diagonal))
    return jnp.concatenate(out, axis=0)


def pack(gram):
    half = gram.shape[0] // 2
    return jnp.concatenate([gram[:half], gram[half:]], axis=1)


def unpack(packed):
    size = packed.shape[1] // 2
    return jnp.concatenate([packed[:, :size], packed[:, size:]], axis=0)


def iterate_kernel(
    plan, peers, current_ref, scale_ref, *refs
):
    tiles = refs[: W + 1]
    out_ref, acc, p_send, p_recv, m_send, m_recv, box = refs[W + 1 : W + 8]
    p_out, p_in, m_out, m_in, send_sem, recv_sem = refs[W + 8 :]
    me = lax.axis_index(AXIS)
    found = peers_of(me, plan)
    barrier = pltpu.get_barrier_semaphore()
    total = 0
    for _, row in found:
        for _, peer in row:
            pl.semaphore_signal(barrier, inc=1, device_id={AXIS: peer}, device_id_type=MESH)
            total += 1
    for offset in range(1, W + 1):

        @pl.when(me >= offset)
        def _():
            pl.semaphore_signal(barrier, inc=1, device_id={AXIS: me - offset}, device_id_type=MESH)

        @pl.when(me + offset < peers)
        def _():
            pl.semaphore_signal(barrier, inc=1, device_id={AXIS: me + offset}, device_id_type=MESH)

    for offset in range(1, W + 1):
        total = total + (me >= offset).astype(jnp.int32) + (me + offset < peers).astype(jnp.int32)
    pl.semaphore_wait(barrier, total)

    def p_copy(step, offset, target):
        return pltpu.make_async_remote_copy(
            src_ref=p_send.at[step],
            dst_ref=p_recv.at[step, offset - 1],
            send_sem=p_out.at[step, offset - 1],
            recv_sem=p_in.at[step, offset - 1],
            device_id={AXIS: target},
            device_id_type=MESH,
        )

    def m_copy(step, offset, target):
        return pltpu.make_async_remote_copy(
            src_ref=m_send.at[step, offset - 1],
            dst_ref=m_recv.at[step, offset - 1],
            send_sem=m_out.at[step, offset - 1],
            recv_sem=m_in.at[step, offset - 1],
            device_id={AXIS: target},
            device_id_type=MESH,
        )

    scale = scale_ref[...]
    out_ref[...] = current_ref[...]
    for step in range(ITERS):
        p_send[step] = (out_ref[...] * scale).astype(jnp.bfloat16)
        for offset in range(1, W + 1):

            @pl.when(me >= offset)
            def _():
                p_copy(step, offset, me - offset).start()

        for offset in range(W, 0, -1):

            @pl.when(me + offset < peers)
            def _():
                m_send[step, offset - 1] = lax.dot_general(
                    p_send[step],
                    tiles[offset][...],
                    (((1,), (0,)), ((), ())),
                    preferred_element_type=jnp.float32,
                )
                m_copy(step, offset, me + offset).start()

        acc[...] = lax.dot_general(
            p_send[step], tiles[0][...], (((1,), (1,)), ((), ())), preferred_element_type=jnp.float32
        )
        for offset in range(1, W + 1):

            @pl.when(me + offset < peers)
            def _():
                p_copy(step, offset, me + offset).wait_recv()
                acc[...] += lax.dot_general(
                    p_recv[step, offset - 1],
                    tiles[offset][...],
                    (((1,), (1,)), ((), ())),
                    preferred_element_type=jnp.float32,
                )

        for offset in range(1, W + 1):

            @pl.when(me >= offset)
            def _():
                m_copy(step, offset, me - offset).wait_recv()
                acc[...] += m_recv[step, offset - 1]

        normed = acc[...] * scale
        gram = lax.dot_general(
            normed, normed, (((1,), (1,)), ((), ())), precision=HIGH, preferred_element_type=jnp.float32
        )
        gram = unpack(
            all_sum(pack(gram), found, box.at[step], send_sem.at[step], recv_sem.at[step])
        )
        inverse = inverse_factor(gram)
        out_ref[...] = lax.dot_general(
            inverse, normed, (((1,), (0,)), ((), ())), precision=HIGH, preferred_element_type=jnp.float32
        )
    for step in range(ITERS):
        for offset in range(1, W + 1):

            @pl.when(me >= offset)
            def _():
                p_copy(step, offset, me - offset).wait_send()

            @pl.when(me + offset < peers)
            def _():
                m_copy(step, offset, me + offset).wait_send()


def iterations(current, scale, tiles, peers):
    size, count = current.shape
    plan = radices(peers)
    phases, widest = len(plan), max(plan)
    dma = pltpu.SemaphoreType.DMA
    return pl.pallas_call(
        functools.partial(iterate_kernel, plan, peers),
        out_shape=jax.ShapeDtypeStruct(current.shape, jnp.float32),
        in_specs=[pl.BlockSpec(memory_space=pltpu.VMEM)] * (W + 3),
        out_specs=pl.BlockSpec(memory_space=pltpu.VMEM),
        scratch_shapes=[
            pltpu.VMEM((size, count), jnp.float32),
            pltpu.VMEM((ITERS, size, count), jnp.bfloat16),
            pltpu.VMEM((ITERS, W, size, count), jnp.bfloat16),
            pltpu.VMEM((ITERS, W, size, count), jnp.float32),
            pltpu.VMEM((ITERS, W, size, count), jnp.float32),
            pltpu.VMEM((ITERS, phases, widest, size // 2, 2 * size), jnp.float32),
            dma((ITERS, W)),
            dma((ITERS, W)),
            dma((ITERS, W)),
            dma((ITERS, W)),
            dma((ITERS, phases, widest)),
            dma((ITERS, phases, widest)),
        ],
        compiler_params=pltpu.CompilerParams(
            collective_id=0, has_side_effects=True, vmem_limit_bytes=48 << 20
        ),
        name="iterations",
    )(current, scale, *tiles)


def shifted(array, axis, by):
    peers = lax.axis_size(axis)
    pairs = [(i, i + by) for i in range(peers) if 0 <= i + by < peers]
    return lax.ppermute(array, axis, pairs)


def unit_rows(features):
    values = features.astype(jnp.float32)
    return (values * lax.rsqrt(jnp.sum(values * values, axis=-1, keepdims=True) + 1e-06)).astype(
        jnp.bfloat16
    )


def affinity(left, right):
    count = left.shape[0]
    step = min(512, count)
    pieces = []
    for start in range(0, count, step):
        scores = lax.dot_general(
            left[start : start + step],
            right,
            (((1,), (1,)), ((), ())),
            preferred_element_type=jnp.float32,
        )
        pieces.append(jnp.exp(scores).astype(jnp.bfloat16))
    return jnp.concatenate(pieces, 0)


def local(peers, features, iterate, band_mask):
    unit = unit_rows(features)
    keep_row = band_mask[0]
    reach = W
    partners = []
    for offset in range(1, reach + 1):
        partners.append(shifted(unit, "rows", -offset))
    tiles = [affinity(unit, unit)]
    for offset in range(1, reach + 1):
        keep = keep_row[offset - 1]
        partner = partners[offset - 1]
        tiles.append(affinity(unit, partner) * keep.astype(jnp.bfloat16))
    degrees = jnp.sum(tiles[0].astype(jnp.float32), axis=1)
    for offset in range(1, reach + 1):
        degrees = degrees + jnp.sum(tiles[offset].astype(jnp.float32), axis=1)
    for offset in range(1, reach + 1):
        column_sums = jnp.sum(tiles[offset].astype(jnp.float32), axis=0)
        degrees = degrees + shifted(column_sums, "rows", offset)
    scale = lax.rsqrt(degrees)[None, :]
    current = iterations(iterate.T, scale, tiles, peers).T
    return (current, degrees)


def solution(mesh):
    return jax.shard_map(
        functools.partial(local, mesh.shape[AXIS]),
        mesh=mesh,
        in_specs=(
            P(("groups", "rows"), None),
            P(("groups", "rows"), None),
            P(("groups", "rows"), None),
        ),
        out_specs=(P(("groups", "rows"), None), P(("groups", "rows"))),
        check_vma=False,
    )
```

```python
import functools

import jax
import jax.numpy as jnp
from jax import lax
from jax.experimental import pallas as pl
from jax.experimental.pallas import tpu as pltpu
from jax.sharding import PartitionSpec as P

W = 2
ITERS = 2
AXIS = "rows"
MESH = pl.DeviceIdType.MESH
HIGH = lax.Precision.HIGHEST


def radices(count):
    out = []
    while count > 1:
        radix = next((r for r in (4, 2, 3, 5, 7) if count % r == 0), count)
        out.append(radix)
        count //= radix
    return out


def peers_of(me, plan):
    stride = 1
    found = []
    for radix in plan:
        digit = lax.rem(lax.div(me, stride), radix)
        row = []
        for k in range(1, radix):
            other = lax.rem(digit + k, radix)
            row.append((other, me + (other - digit) * stride))
        found.append((digit, row))
        stride *= radix
    return found


def all_sum(value, found, box, send_sem, recv_sem):
    for phase, (digit, row) in enumerate(found):
        box[phase, digit] = value
        copies = []
        for k, (other, peer) in enumerate(row):
            copy = pltpu.make_async_remote_copy(
                src_ref=box.at[phase, digit],
                dst_ref=box.at[phase, digit],
                send_sem=send_sem.at[phase, k],
                recv_sem=recv_sem.at[phase, digit],
                device_id={AXIS: peer},
                device_id_type=MESH,
            )
            copy.start()
            copies.append(copy)
        for other, peer in row:
            pltpu.make_async_remote_copy(
                src_ref=box.at[phase, other],
                dst_ref=box.at[phase, other],
                send_sem=send_sem.at[phase, 0],
                recv_sem=recv_sem.at[phase, other],
                device_id={AXIS: peer},
                device_id_type=MESH,
            ).wait_recv()
        value = box[phase, 0]
        for slot in range(1, len(row) + 1):
            value = value + box[phase, slot]
        for copy in copies:
            copy.wait_send()
    return value


def inverse_factor(gram):
    size = gram.shape[0]
    rows = lax.broadcasted_iota(jnp.int32, (size, size), 0)
    cols = lax.broadcasted_iota(jnp.int32, (size, size), 1)
    both = jnp.concatenate([gram, jnp.where(rows == cols, 1.0, 0.0)], axis=1)
    count = size // 8
    bands = [both[8 * b : 8 * b + 8] for b in range(count)]
    sub = lax.broadcasted_iota(jnp.int32, (8, 1), 0)
    pivots = []
    for j in range(0, size, 2):
        b, s = j // 8, j % 8
        first, second = bands[b][s : s + 1], bands[b][s + 1 : s + 2]
        pivot = first[:, j : j + 1]
        first_scaled = first * (1.0 / pivot)
        reduced = second - second[:, j : j + 1] * first_scaled
        after = reduced[:, j + 1 : j + 2]
        second_scaled = reduced * (1.0 / after)
        coupling = first_scaled[:, j + 1 : j + 2]
        pivots += [pivot, after]
        for c in range(b, count):
            left = bands[c][:, j : j + 1]
            right = bands[c][:, j + 1 : j + 2] - left * coupling
            if c == b:
                left = jnp.where(sub > s, left, 0.0)
                right = jnp.where(sub > s + 1, right, 0.0)
            bands[c] = bands[c] - left * first_scaled - right * second_scaled
    out = []
    for b in range(count):
        diagonal = jnp.zeros((8, 1), jnp.float32)
        for s in range(8):
            diagonal = jnp.where(sub == s, pivots[8 * b + s], diagonal)
        out.append(bands[b][:, size:] * lax.rsqrt(diagonal))
    return jnp.concatenate(out, axis=0)


def pack(gram):
    half = gram.shape[0] // 2
    return jnp.concatenate([gram[:half], gram[half:]], axis=1)


def unpack(packed):
    size = packed.shape[1] // 2
    return jnp.concatenate([packed[:, :size], packed[:, size:]], axis=0)


def iterate_kernel(
    plan, peers, current_ref, scale_ref, *refs
):
    tiles = refs[: W + 1]
    out_ref, acc, p_send, p_recv, m_send, m_recv, box = refs[W + 1 : W + 8]
    p_out, p_in, m_out, m_in, send_sem, recv_sem = refs[W + 8 :]
    me = lax.axis_index(AXIS)
    found = peers_of(me, plan)
    barrier = pltpu.get_barrier_semaphore()
    total = 0
    for _, row in found:
        for _, peer in row:
            pl.semaphore_signal(barrier, inc=1, device_id={AXIS: peer}, device_id_type=MESH)
            total += 1
    for offset in range(1, W + 1):

        @pl.when(me >= offset)
        def _():
            pl.semaphore_signal(barrier, inc=1, device_id={AXIS: me - offset}, device_id_type=MESH)

        @pl.when(me + offset < peers)
        def _():
            pl.semaphore_signal(barrier, inc=1, device_id={AXIS: me + offset}, device_id_type=MESH)

    for offset in range(1, W + 1):
        total = total + (me >= offset).astype(jnp.int32) + (me + offset < peers).astype(jnp.int32)
    pl.semaphore_wait(barrier, total)

    def p_copy(step, offset, target):
        return pltpu.make_async_remote_copy(
            src_ref=p_send.at[step],
            dst_ref=p_recv.at[step, offset - 1],
            send_sem=p_out.at[step, offset - 1],
            recv_sem=p_in.at[step, offset - 1],
            device_id={AXIS: target},
            device_id_type=MESH,
        )

    def m_copy(step, offset, target):
        return pltpu.make_async_remote_copy(
            src_ref=m_send.at[step, offset - 1],
            dst_ref=m_recv.at[step, offset - 1],
            send_sem=m_out.at[step, offset - 1],
            recv_sem=m_in.at[step, offset - 1],
            device_id={AXIS: target},
            device_id_type=MESH,
        )

    scale = scale_ref[...]
    out_ref[...] = current_ref[...]
    for step in range(ITERS):
        p_send[step] = (out_ref[...] * scale).astype(jnp.bfloat16)
        for offset in range(1, W + 1):

            @pl.when(me >= offset)
            def _():
                p_copy(step, offset, me - offset).start()

        for offset in range(W, 0, -1):

            @pl.when(me + offset < peers)
            def _():
                m_send[step, offset - 1] = lax.dot_general(
                    p_send[step],
                    tiles[offset][...],
                    (((1,), (0,)), ((), ())),
                    preferred_element_type=jnp.float32,
                )
                m_copy(step, offset, me + offset).start()

        acc[...] = lax.dot_general(
            p_send[step], tiles[0][...], (((1,), (1,)), ((), ())), preferred_element_type=jnp.float32
        )
        for offset in range(1, W + 1):

            @pl.when(me + offset < peers)
            def _():
                p_copy(step, offset, me + offset).wait_recv()
                acc[...] += lax.dot_general(
                    p_recv[step, offset - 1],
                    tiles[offset][...],
                    (((1,), (1,)), ((), ())),
                    preferred_element_type=jnp.float32,
                )

        for offset in range(1, W + 1):

            @pl.when(me >= offset)
            def _():
                m_copy(step, offset, me - offset).wait_recv()
                acc[...] += m_recv[step, offset - 1]

        normed = acc[...] * scale
        gram = lax.dot_general(
            normed, normed, (((1,), (1,)), ((), ())), precision=HIGH, preferred_element_type=jnp.float32
        )
        gram = unpack(
            all_sum(pack(gram), found, box.at[step], send_sem.at[step], recv_sem.at[step])
        )
        inverse = inverse_factor(gram)
        out_ref[...] = lax.dot_general(
            inverse, normed, (((1,), (0,)), ((), ())), precision=HIGH, preferred_element_type=jnp.float32
        )
    for step in range(ITERS):
        for offset in range(1, W + 1):

            @pl.when(me >= offset)
            def _():
                p_copy(step, offset, me - offset).wait_send()

            @pl.when(me + offset < peers)
            def _():
                m_copy(step, offset, me + offset).wait_send()


def iterations(current, scale, tiles, peers):
    size, count = current.shape
    plan = radices(peers)
    phases, widest = len(plan), max(plan)
    dma = pltpu.SemaphoreType.DMA
    return pl.pallas_call(
        functools.partial(iterate_kernel, plan, peers),
        out_shape=jax.ShapeDtypeStruct(current.shape, jnp.float32),
        in_specs=[pl.BlockSpec(memory_space=pltpu.VMEM)] * (W + 3),
        out_specs=pl.BlockSpec(memory_space=pltpu.VMEM),
        scratch_shapes=[
            pltpu.VMEM((size, count), jnp.float32),
            pltpu.VMEM((ITERS, size, count), jnp.bfloat16),
            pltpu.VMEM((ITERS, W, size, count), jnp.bfloat16),
            pltpu.VMEM((ITERS, W, size, count), jnp.float32),
            pltpu.VMEM((ITERS, W, size, count), jnp.float32),
            pltpu.VMEM((ITERS, phases, widest, size // 2, 2 * size), jnp.float32),
            dma((ITERS, W)),
            dma((ITERS, W)),
            dma((ITERS, W)),
            dma((ITERS, W)),
            dma((ITERS, phases, widest)),
            dma((ITERS, phases, widest)),
        ],
        compiler_params=pltpu.CompilerParams(
            collective_id=0, has_side_effects=True, vmem_limit_bytes=48 << 20
        ),
        name="iterations",
    )(current, scale, *tiles)


def shifted(array, axis, by):
    peers = lax.axis_size(axis)
    pairs = [(i, i + by) for i in range(peers) if 0 <= i + by < peers]
    return lax.ppermute(array, axis, pairs)


def unit_rows(features):
    values = features.astype(jnp.float32)
    return (values * lax.rsqrt(jnp.sum(values * values, axis=-1, keepdims=True) + 1e-06)).astype(
        jnp.bfloat16
    )


def affinity(left, right):
    count = left.shape[0]
    step = min(512, count)
    pieces = []
    for start in range(0, count, step):
        scores = lax.dot_general(
            left[start : start + step],
            right,
            (((1,), (1,)), ((), ())),
            preferred_element_type=jnp.float32,
        )
        pieces.append(jnp.exp(scores).astype(jnp.bfloat16))
    return jnp.concatenate(pieces, 0)


def local(peers, features, iterate, band_mask):
    unit = unit_rows(features)
    keep_row = band_mask[0]
    reach = W
    nearest = shifted(unit, "rows", -1)
    direct = lax.ppermute(unit, "rows", [(i + 2, i) for i in range(1, peers - 2, 2)])
    relayed = lax.ppermute(nearest, "rows", [(i + 1, i) for i in range(0, peers - 2, 2)])
    partners = [nearest, jnp.where(lax.rem(lax.axis_index("rows"), 2) == 0, relayed, direct)]
    tiles = [affinity(unit, unit)]
    for offset in range(1, reach + 1):
        keep = keep_row[offset - 1]
        partner = partners[offset - 1]
        tiles.append(affinity(unit, partner) * keep.astype(jnp.bfloat16))
    degrees = jnp.sum(tiles[0].astype(jnp.float32), axis=1)
    for offset in range(1, reach + 1):
        degrees = degrees + jnp.sum(tiles[offset].astype(jnp.float32), axis=1)
    for offset in range(1, reach + 1):
        column_sums = jnp.sum(tiles[offset].astype(jnp.float32), axis=0)
        degrees = degrees + shifted(column_sums, "rows", offset)
    scale = lax.rsqrt(degrees)[None, :]
    current = iterations(iterate.T, scale, tiles, peers).T
    return (current, degrees)


def solution(mesh):
    return jax.shard_map(
        functools.partial(local, mesh.shape[AXIS]),
        mesh=mesh,
        in_specs=(
            P(("groups", "rows"), None),
            P(("groups", "rows"), None),
            P(("groups", "rows"), None),
        ),
        out_specs=(P(("groups", "rows"), None), P(("groups", "rows"))),
        check_vma=False,
    )
```

```python
import functools

import jax
import jax.numpy as jnp
from jax import lax
from jax.experimental import pallas as pl
from jax.experimental.pallas import tpu as pltpu
from jax.sharding import PartitionSpec as P

W = 2
ITERS = 2
AXIS = "rows"
MESH = pl.DeviceIdType.MESH
HIGH = lax.Precision.HIGHEST


def radices(count):
    out = []
    while count > 1:
        radix = next((r for r in (4, 2, 3, 5, 7) if count % r == 0), count)
        out.append(radix)
        count //= radix
    return out


def peers_of(me, plan):
    stride = 1
    found = []
    for radix in plan:
        digit = lax.rem(lax.div(me, stride), radix)
        row = []
        for k in range(1, radix):
            other = lax.rem(digit + k, radix)
            row.append((other, me + (other - digit) * stride))
        found.append((digit, row))
        stride *= radix
    return found


def all_sum(value, found, box, send_sem, recv_sem):
    for phase, (digit, row) in enumerate(found):
        box[phase, digit] = value
        copies = []
        for k, (other, peer) in enumerate(row):
            copy = pltpu.make_async_remote_copy(
                src_ref=box.at[phase, digit],
                dst_ref=box.at[phase, digit],
                send_sem=send_sem.at[phase, k],
                recv_sem=recv_sem.at[phase, digit],
                device_id={AXIS: peer},
                device_id_type=MESH,
            )
            copy.start()
            copies.append(copy)
        for other, peer in row:
            pltpu.make_async_remote_copy(
                src_ref=box.at[phase, other],
                dst_ref=box.at[phase, other],
                send_sem=send_sem.at[phase, 0],
                recv_sem=recv_sem.at[phase, other],
                device_id={AXIS: peer},
                device_id_type=MESH,
            ).wait_recv()
        value = box[phase, 0]
        for slot in range(1, len(row) + 1):
            value = value + box[phase, slot]
        for copy in copies:
            copy.wait_send()
    return value


def inverse_factor(gram):
    size = gram.shape[0]
    rows = lax.broadcasted_iota(jnp.int32, (size, size), 0)
    cols = lax.broadcasted_iota(jnp.int32, (size, size), 1)
    both = jnp.concatenate([gram, jnp.where(rows == cols, 1.0, 0.0)], axis=1)
    count = size // 8
    bands = [both[8 * b : 8 * b + 8] for b in range(count)]
    sub = lax.broadcasted_iota(jnp.int32, (8, 1), 0)
    pivots = []
    for j in range(size):
        b, s = j // 8, j % 8
        row = bands[b][s : s + 1]
        pivot = row[:, j : j + 1]
        pivots.append(pivot)
        scaled = row * (1.0 / pivot)
        for c in range(b, count):
            column = bands[c][:, j : j + 1]
            if c == b:
                column = jnp.where(sub > s, column, 0.0)
            bands[c] = bands[c] - column * scaled
    out = []
    for b in range(count):
        diagonal = jnp.zeros((8, 1), jnp.float32)
        for s in range(8):
            diagonal = jnp.where(sub == s, pivots[8 * b + s], diagonal)
        out.append(bands[b][:, size:] * lax.rsqrt(diagonal))
    return jnp.concatenate(out, axis=0)


def pack(gram):
    half = gram.shape[0] // 2
    return jnp.concatenate([gram[:half], gram[half:]], axis=1)


def unpack(packed):
    size = packed.shape[1] // 2
    return jnp.concatenate([packed[:, :size], packed[:, size:]], axis=0)


def iterate_kernel(
    plan, peers, current_ref, scale_ref, *refs
):
    tiles = refs[: W + 1]
    out_ref, acc, p_send, p_recv, m_send, m_recv, box = refs[W + 1 : W + 8]
    p_out, p_in, m_out, m_in, send_sem, recv_sem = refs[W + 8 :]
    me = lax.axis_index(AXIS)
    found = peers_of(me, plan)
    barrier = pltpu.get_barrier_semaphore()
    total = 0
    for _, row in found:
        for _, peer in row:
            pl.semaphore_signal(barrier, inc=1, device_id={AXIS: peer}, device_id_type=MESH)
            total += 1
    for offset in range(1, W + 1):

        @pl.when(me >= offset)
        def _():
            pl.semaphore_signal(barrier, inc=1, device_id={AXIS: me - offset}, device_id_type=MESH)

        @pl.when(me + offset < peers)
        def _():
            pl.semaphore_signal(barrier, inc=1, device_id={AXIS: me + offset}, device_id_type=MESH)

    for offset in range(1, W + 1):
        total = total + (me >= offset).astype(jnp.int32) + (me + offset < peers).astype(jnp.int32)
    pl.semaphore_wait(barrier, total)

    def p_copy(step, offset, target):
        return pltpu.make_async_remote_copy(
            src_ref=p_send.at[step],
            dst_ref=p_recv.at[step, offset - 1],
            send_sem=p_out.at[step, offset - 1],
            recv_sem=p_in.at[step, offset - 1],
            device_id={AXIS: target},
            device_id_type=MESH,
        )

    def m_copy(step, offset, target):
        return pltpu.make_async_remote_copy(
            src_ref=m_send.at[step, offset - 1],
            dst_ref=m_recv.at[step, offset - 1],
            send_sem=m_out.at[step, offset - 1],
            recv_sem=m_in.at[step, offset - 1],
            device_id={AXIS: target},
            device_id_type=MESH,
        )

    scale = scale_ref[...]
    out_ref[...] = current_ref[...]
    for step in range(ITERS):
        p_send[step] = (out_ref[...] * scale).astype(jnp.bfloat16)
        for offset in range(1, W + 1):

            @pl.when(me >= offset)
            def _():
                p_copy(step, offset, me - offset).start()

        for offset in range(W, 0, -1):

            @pl.when(me + offset < peers)
            def _():
                m_send[step, offset - 1] = lax.dot_general(
                    p_send[step],
                    tiles[offset][...],
                    (((1,), (0,)), ((), ())),
                    preferred_element_type=jnp.float32,
                )
                m_copy(step, offset, me + offset).start()

        acc[...] = lax.dot_general(
            p_send[step], tiles[0][...], (((1,), (1,)), ((), ())), preferred_element_type=jnp.float32
        )
        for offset in range(1, W + 1):

            @pl.when(me + offset < peers)
            def _():
                p_copy(step, offset, me + offset).wait_recv()
                acc[...] += lax.dot_general(
                    p_recv[step, offset - 1],
                    tiles[offset][...],
                    (((1,), (1,)), ((), ())),
                    preferred_element_type=jnp.float32,
                )

        for offset in range(1, W + 1):

            @pl.when(me >= offset)
            def _():
                m_copy(step, offset, me - offset).wait_recv()
                acc[...] += m_recv[step, offset - 1]

        normed = acc[...] * scale
        gram = lax.dot_general(
            normed, normed, (((1,), (1,)), ((), ())), precision=HIGH, preferred_element_type=jnp.float32
        )
        gram = unpack(
            all_sum(pack(gram), found, box.at[step], send_sem.at[step], recv_sem.at[step])
        )
        inverse = inverse_factor(gram)
        out_ref[...] = lax.dot_general(
            inverse, normed, (((1,), (0,)), ((), ())), precision=HIGH, preferred_element_type=jnp.float32
        )
    for step in range(ITERS):
        for offset in range(1, W + 1):

            @pl.when(me >= offset)
            def _():
                p_copy(step, offset, me - offset).wait_send()

            @pl.when(me + offset < peers)
            def _():
                m_copy(step, offset, me + offset).wait_send()


def iterations(current, scale, tiles, peers):
    size, count = current.shape
    plan = radices(peers)
    phases, widest = len(plan), max(plan)
    dma = pltpu.SemaphoreType.DMA
    return pl.pallas_call(
        functools.partial(iterate_kernel, plan, peers),
        out_shape=jax.ShapeDtypeStruct(current.shape, jnp.float32),
        in_specs=[pl.BlockSpec(memory_space=pltpu.VMEM)] * (W + 3),
        out_specs=pl.BlockSpec(memory_space=pltpu.VMEM),
        scratch_shapes=[
            pltpu.VMEM((size, count), jnp.float32),
            pltpu.VMEM((ITERS, size, count), jnp.bfloat16),
            pltpu.VMEM((ITERS, W, size, count), jnp.bfloat16),
            pltpu.VMEM((ITERS, W, size, count), jnp.float32),
            pltpu.VMEM((ITERS, W, size, count), jnp.float32),
            pltpu.VMEM((ITERS, phases, widest, size // 2, 2 * size), jnp.float32),
            dma((ITERS, W)),
            dma((ITERS, W)),
            dma((ITERS, W)),
            dma((ITERS, W)),
            dma((ITERS, phases, widest)),
            dma((ITERS, phases, widest)),
        ],
        compiler_params=pltpu.CompilerParams(
            collective_id=0, has_side_effects=True, vmem_limit_bytes=48 << 20
        ),
        name="iterations",
    )(current, scale, *tiles)


def shifted(array, axis, by):
    peers = lax.axis_size(axis)
    pairs = [(i, i + by) for i in range(peers) if 0 <= i + by < peers]
    return lax.ppermute(array, axis, pairs)


def unit_rows(features):
    values = features.astype(jnp.float32)
    return (values * lax.rsqrt(jnp.sum(values * values, axis=-1, keepdims=True) + 1e-06)).astype(
        jnp.bfloat16
    )


def affinity(left, right):
    count = left.shape[0]
    step = min(512, count)
    pieces = []
    for start in range(0, count, step):
        scores = lax.dot_general(
            left[start : start + step],
            right,
            (((1,), (1,)), ((), ())),
            preferred_element_type=jnp.float32,
        )
        pieces.append(jnp.exp(scores).astype(jnp.bfloat16))
    return jnp.concatenate(pieces, 0)


def local(peers, features, iterate, band_mask):
    unit = unit_rows(features)
    keep_row = band_mask[0]
    reach = W
    nearest = shifted(unit, "rows", -1)
    direct = lax.ppermute(unit, "rows", [(i + 2, i) for i in range(1, peers - 2, 2)])
    relayed = lax.ppermute(nearest, "rows", [(i + 1, i) for i in range(0, peers - 2, 2)])
    partners = [nearest, jnp.where(lax.rem(lax.axis_index("rows"), 2) == 0, relayed, direct)]
    tiles = [affinity(unit, unit)]
    for offset in range(1, reach + 1):
        keep = keep_row[offset - 1]
        partner = partners[offset - 1]
        tiles.append(affinity(unit, partner) * keep.astype(jnp.bfloat16))
    degrees = jnp.sum(tiles[0].astype(jnp.float32), axis=1)
    for offset in range(1, reach + 1):
        degrees = degrees + jnp.sum(tiles[offset].astype(jnp.float32), axis=1)
    for offset in range(1, reach + 1):
        column_sums = jnp.sum(tiles[offset].astype(jnp.float32), axis=0)
        degrees = degrees + shifted(column_sums, "rows", offset)
    scale = lax.rsqrt(degrees)[None, :]
    current = iterations(iterate.T, scale, tiles, peers).T
    return (current, degrees)


def solution(mesh):
    return jax.shard_map(
        functools.partial(local, mesh.shape[AXIS]),
        mesh=mesh,
        in_specs=(
            P(("groups", "rows"), None),
            P(("groups", "rows"), None),
            P(("groups", "rows"), None),
        ),
        out_specs=(P(("groups", "rows"), None), P(("groups", "rows"))),
        check_vma=False,
    )
```
